512 devices in a mesh: px: 64 (over z, x), pz: 8 (over y, core).
Axes of the slice: x: 4, y: 4, z: 16, core: 2. Of those that a mesh axis runs over, the one named last changes fastest.
Arguments:
- velocity: float32 [3, 512, 512, 128], P(None, 'pz', 'px'), may hold values from -6 to 6
- metric_first: float32 [512], replicated, may hold values from 0.5 to 2
- metric_second: float32 [512], replicated, may hold values from -4 to 4
Outputs:
- tendency: float32 [3, 512, 512, 128], P(None, 'pz', 'px')
The draws below stay inside these ranges and needn't reach their ends.
All inputs are finite; a program needn't handle non-finite values.
Results may differ from the reference program's by a relative error of at most 0.0003.
Values sent between devices are 32-bit elements; how exact they have to be, the bound alone decides.
No kernel may reach another device: no remote copies, remote signals or barrier semaphores. Data moves between devices by JAX's collectives and lax.ppermute only.
A program may use at most 64 MiB of HBM per device.

```python
import math
import jax
import jax.numpy as jnp
from jax import lax

NY = 512
ZW = 128
NX = 512


def block_levels(stream_key, shape, shards, least, top_value):
    loudness = 1.0
    for dim, parts in shards:
        draws = jax.random.uniform(jax.random.fold_in(jax.random.fold_in(stream_key, 6), dim), (parts,), jnp.float32, least / len(shards), top_value / len(shards))
        loudness = loudness * jnp.repeat(jnp.exp(draws), shape[dim] // parts).reshape((-1,) + (1,) * (len(shape) - 1 - dim))
    return loudness


def scatter_about(key, shape, scale, most, shards=(), dtype=jnp.bfloat16):
    values = scale * jax.random.normal(key, shape, jnp.float32)
    if shards:
        values = values * block_levels(key, shape, shards, -0.22, 0.18)
    return jnp.clip(values, -most, most).astype(dtype)


def setup_inputs(seed: int = 0) -> dict:
    keys = jax.random.split(jax.random.key(seed), 4)
    return {
        "velocity": scatter_about(keys[0], (3, NY, NX, ZW), 1.0, 6.0, ((1, 8), (2, 64)), jnp.float32),
        "metric_first": jnp.clip(jnp.exp(jax.random.uniform(keys[1], (NY,), jnp.float32, math.log(0.5), math.log(2.0))), 0.5, 2.0),
        "metric_second": scatter_about(keys[2], (NY,), 1.0, 4.0, (), jnp.float32),
    }


FIRST_ALPHA = 0.4998
FIRST_NEAR = 2.0 * (FIRST_ALPHA + 2.0) / 3.0
FIRST_FAR = (4.0 * FIRST_ALPHA - 1.0) / 3.0
SECOND_ALPHA = 2.0 / 11.0
SECOND_NEAR = 12.0 / 11.0
SECOND_FAR = 3.0 / 11.0
VISCOSITY = 0.5

def first_terms(minus_two, minus_one, plus_one, plus_two):
    return FIRST_NEAR * 0.5 * (plus_one - minus_one) + FIRST_FAR * 0.25 * (plus_two - minus_two)

def second_terms(minus_two, minus_one, center, plus_one, plus_two):
    return SECOND_NEAR * (plus_one - 2.0 * center + minus_one) + SECOND_FAR * 0.25 * (plus_two - 2.0 * center + minus_two)

def band_arrays(alpha_value, length):
    places = jnp.arange(length)
    lower_band = jnp.where(places == 0, 0.0, alpha_value).astype(jnp.float32)
    upper_band = jnp.where(places == length - 1, 0.0, alpha_value).astype(jnp.float32)
    middle = jnp.ones((length,), jnp.float32)
    return (lower_band, middle, upper_band)

def reference(velocity, metric_first, metric_second):
    count_y = velocity.shape[1]
    count_x = velocity.shape[2]
    wave_numbers = jnp.arange(count_x // 2 + 1).astype(jnp.float32)
    angle_table = jnp.cos(2.0 * math.pi * wave_numbers / count_x)
    symbol_one = (1.0 + 2.0 * FIRST_ALPHA * angle_table)[None, :, None]
    symbol_two = (1.0 + 2.0 * SECOND_ALPHA * angle_table)[None, :, None]
    lower_one, middle, upper_one = band_arrays(FIRST_ALPHA, count_y)
    lower_two, middle, upper_two = band_arrays(SECOND_ALPHA, count_y)
    scale_rows = metric_first[:, None, None]
    curve_rows = metric_second[:, None, None]
    results = []
    for member in range(3):
        component_field = velocity[member]
        nearby = [jnp.roll(component_field, offset, axis=1) for offset in (2, 1, 0, -1, -2)]
        first_x = first_terms(nearby[0], nearby[1], nearby[3], nearby[4])
        second_x = second_terms(nearby[0], nearby[1], nearby[2], nearby[3], nearby[4])
        deriv_x_one = jnp.fft.irfft(jnp.fft.rfft(first_x, axis=1) / symbol_one, n=count_x, axis=1)
        deriv_x_two = jnp.fft.irfft(jnp.fft.rfft(second_x, axis=1) / symbol_two, n=count_x, axis=1)
        padded = jnp.pad(component_field, ((2, 2), (0, 0), (0, 0)))
        rows_near = [padded[offset:offset + count_y] for offset in range(5)]
        first_y = first_terms(rows_near[0], rows_near[1], rows_near[3], rows_near[4])
        second_y = second_terms(rows_near[0], rows_near[1], rows_near[2], rows_near[3], rows_near[4])
        eta_one = lax.linalg.tridiagonal_solve(lower_one, middle, upper_one, first_y.reshape(count_y, -1)).reshape(component_field.shape)
        eta_two = lax.linalg.tridiagonal_solve(lower_two, middle, upper_two, second_y.reshape(count_y, -1)).reshape(component_field.shape)
        deriv_y_one = scale_rows * eta_one
        deriv_y_two = scale_rows * scale_rows * eta_two + curve_rows * eta_one
        tendency_part = -(velocity[0] * deriv_x_one + velocity[1] * deriv_y_one) + VISCOSITY * (deriv_x_two + deriv_y_two)
        results.append(tendency_part.astype(jnp.float32))
    return jnp.stack(results)
```

```python
import math

import jax
import jax.numpy as jnp
import numpy as np
from jax import lax
from jax.experimental import pallas as pl
from jax.experimental.pallas import tpu as pltpu
from jax.sharding import PartitionSpec as P

FIRST_ALPHA = 0.4998
FIRST_NEAR = 2.0 * (FIRST_ALPHA + 2.0) / 3.0
FIRST_FAR = (4.0 * FIRST_ALPHA - 1.0) / 3.0
SECOND_ALPHA = 2.0 / 11.0
SECOND_NEAR = 12.0 / 11.0
SECOND_FAR = 3.0 / 11.0
VISCOSITY = 0.5

COMPS = 3
YB = 64
XB = 8
LANES = 128
ROWS = COMPS * YB
GROUP = 8
PART = ROWS // GROUP
YROWS = COMPS * XB


class Line:
    def __init__(self, alpha, stencil, sign):
        root = math.sqrt(1.0 - 4.0 * alpha * alpha)
        self.r = -2.0 * alpha / (1.0 + root)
        green = [self.r ** abs(n) / root for n in range(-4, 5)]
        reply = [sum(stencil[k + 2] * green[n + k + 4] for k in range(-2, 3)) for n in (0, 1, 2)]
        self.sign = sign
        self.mid = reply[0]
        self.up = reply[2] / self.r**2
        self.near = reply[1] - self.up * self.r


ONE = Line(
    FIRST_ALPHA,
    [-FIRST_FAR / 4, -FIRST_NEAR / 2, 0.0, FIRST_NEAR / 2, FIRST_FAR / 4],
    -1.0,
)
TWO = Line(
    SECOND_ALPHA,
    [
        SECOND_FAR / 4,
        SECOND_NEAR,
        -2.0 * SECOND_NEAR - SECOND_FAR / 2,
        SECOND_NEAR,
        SECOND_FAR / 4,
    ],
    1.0,
)
LINES = (ONE, TWO)


def ring_table(groups, cells):
    table = np.zeros((groups, 4 * groups))
    for q in range(groups):
        for s, line in enumerate(LINES):
            sigma = line.r**cells
            for d in range(1, groups + 1):
                weight = sigma ** (d - 1) / (1.0 - sigma**groups)
                table[q, (2 * s) * groups + (q - d) % groups] += weight
                table[q, (2 * s + 1) * groups + (q + d) % groups] += weight
    return table.astype(np.float32)


def wall_table(blocks, cells):
    table = np.zeros((blocks, 8 * blocks + 8))
    for s, line in enumerate(LINES):
        rho = line.r**cells
        eps = line.r ** (blocks * cells + 1)
        up, down = line.up, line.sign * line.up
        below = np.array([down * line.r * rho**j for j in range(blocks)])
        above = np.array([up * line.r * rho ** (blocks - 1 - j) for j in range(blocks)])
        scale = -1.0 / (1.0 - eps * eps)
        for k in range(blocks):
            low_plus = np.array([rho ** (k - 1 - j) if j < k else 0.0 for j in range(blocks)])
            high_minus = np.array([rho ** (j - k - 1) if j > k else 0.0 for j in range(blocks)])
            low_plus = low_plus - scale * eps * above * rho**k / up
            low_minus = scale * below * rho**k / up
            high_plus = scale * above * rho ** (blocks - 1 - k) / down
            high_minus = high_minus - scale * eps * below * rho ** (blocks - 1 - k) / down
            for m, row in enumerate((low_plus, low_minus, high_plus, high_minus)):
                for j in range(blocks):
                    table[k, (4 * s + m) * blocks + j] = row[((k - j // 2 * 2) % blocks) ^ (j % 2)]
        table[0, 8 * blocks + s] = line.near / (line.up * line.r)
        table[blocks - 1, 8 * blocks + 2 + s] = line.near / (line.up * line.r)
    table[1:, 8 * blocks + 4] = 1.0
    table[:-1, 8 * blocks + 5] = 1.0
    return table.astype(np.float32)


def plane(base, index):
    return pl.ds(base + index, 8, stride=XB)


def moments_x(v_ref, out_ref):
    for g in range(ROWS // 8):
        sums = [None] * 4
        for i in range(XB):
            f = v_ref[plane(64 * g, i), :]
            for s, line in enumerate(LINES):
                sums[2 * s] = f if i == 0 else sums[2 * s] * line.r + f
                sums[2 * s + 1] = f if i == 0 else sums[2 * s + 1] + line.r**i * f
        part, at = divmod(8 * g, PART)
        for m in range(4):
            out_ref[part, m * PART + at : m * PART + at + 8, :] = sums[m]


def moments_y(place_ref, table_ref, v_ref, here_ref, low_ref, high_ref):
    k = place_ref[1]
    base = 8 * table_ref.shape[0]
    for c in range(COMPS):
        sums = [None] * 4
        first = v_ref[c * YB * XB : c * YB * XB + XB, :]
        for y in range(YB):
            f = v_ref[(c * YB + y) * XB : (c * YB + y + 1) * XB, :]
            for s, line in enumerate(LINES):
                sums[2 * s] = f if y == 0 else sums[2 * s] * line.r + f
                sums[2 * s + 1] = f if y == 0 else sums[2 * s + 1] + line.r**y * f
        last = f
        for s in range(2):
            sums[2 * s] = sums[2 * s] + table_ref[k, base + 2 + s] * last
            sums[2 * s + 1] = sums[2 * s + 1] + table_ref[k, base + s] * first
        for m, value in enumerate((*sums, last, first)):
            here_ref[m * YROWS + c * XB : m * YROWS + (c + 1) * XB, :] = value
    for g in range(ROWS // 8):
        low_ref[8 * g : 8 * g + 8, :] = v_ref[plane(64 * g, 0), :]
        high_ref[8 * g : 8 * g + 8, :] = v_ref[plane(64 * g, XB - 1), :]


def pair_up(here_ref, partner_ref, *out_refs):
    for ref in out_refs:
        ref[0 : 4 * YROWS, :] = here_ref[0 : 4 * YROWS, :]
        ref[4 * YROWS : 8 * YROWS, :] = partner_ref[0 : 4 * YROWS, :]
    out_refs[0][8 * YROWS : 9 * YROWS, :] = partner_ref[4 * YROWS : 5 * YROWS, :]
    out_refs[-1][8 * YROWS : 9 * YROWS, :] = partner_ref[5 * YROWS : 6 * YROWS, :]


def group_moments(near_ref, out_ref):
    for s, line in enumerate(LINES):
        rho = line.r**XB
        up = near_ref[0, 2 * s * PART : (2 * s + 1) * PART, :]
        down = near_ref[GROUP - 1, (2 * s + 1) * PART : (2 * s + 2) * PART, :]
        for j in range(1, GROUP):
            up = up * rho + near_ref[j, 2 * s * PART : (2 * s + 1) * PART, :]
            down = down * rho + near_ref[GROUP - 1 - j, (2 * s + 1) * PART : (2 * s + 2) * PART, :]
        for j in range(out_ref.shape[0]):
            out_ref[j, 2 * s * PART : (2 * s + 1) * PART, :] = up
            out_ref[j, (2 * s + 1) * PART : (2 * s + 2) * PART, :] = down


def entering(place_ref, table_ref, near_ref, far_ref, out_ref):
    q = place_ref[0]
    groups = far_ref.shape[0]
    for s, line in enumerate(LINES):
        rho = line.r**XB
        for side in range(2):
            at = (2 * s + side) * PART
            total = table_ref[q, (2 * s + side) * groups] * far_ref[0, at : at + PART, :]
            for j in range(1, groups):
                weight = table_ref[q, (2 * s + side) * groups + j]
                total = total + weight * far_ref[j, at : at + PART, :]
            for j in range(GROUP):
                here = j if side == 0 else GROUP - 1 - j
                out_ref[here, at : at + PART, :] = total
                if j < GROUP - 1:
                    total = total * rho + near_ref[here, at : at + PART, :]


def local_terms(place_ref, table_ref, first_ref, second_ref, v_ref, low_ref, high_ref, *refs):
    *wall_refs, acc_ref, u_ref, run_ref, y_ref = refs
    k = place_ref[1]
    here_ref, partner_ref, *pair_refs = wall_refs
    blocks = table_ref.shape[0]
    wall = [here_ref, partner_ref]
    for pair_ref in pair_refs:
        wall += [pair_ref.at[0 : 4 * YROWS], pair_ref.at[4 * YROWS : 8 * YROWS]]
    base = 8 * blocks
    starts = []
    for s in range(2):
        for side in range(2):
            total = None
            for sign in range(2):
                at = (2 * s + sign) * YROWS
                for j in range(blocks):
                    weight = table_ref[k, (4 * s + 2 * side + sign) * blocks + j]
                    term = weight * wall[j][at : at + YROWS, :]
                    total = term if total is None else total + term
            starts.append(total)
    odd = k % 2 == 1
    lasts = (partner_ref[4 * YROWS : 5 * YROWS, :], pair_refs[0][8 * YROWS : 9 * YROWS, :])
    firsts = (pair_refs[-1][8 * YROWS : 9 * YROWS, :], partner_ref[5 * YROWS : 6 * YROWS, :])
    rows_below = jnp.where(odd, *lasts) * table_ref[k, base + 4]
    rows_above = jnp.where(odd, *firsts) * table_ref[k, base + 5]

    def pick(total):
        return tuple(total[c * XB : (c + 1) * XB] for c in range(COMPS))

    def at(c, y):
        return pl.ds(pl.multiple_of((c * YB + y) * XB, XB), XB)

    def up(y, carry):
        ones, twos = carry
        new_one, new_two = [], []
        for c in range(COMPS):
            run_ref[0, at(c, y), :] = ones[c]
            run_ref[1, at(c, y), :] = twos[c]
            f = v_ref[at(c, y), :]
            new_one.append(ones[c] * ONE.r + f)
            new_two.append(twos[c] * TWO.r + f)
        return (tuple(new_one), tuple(new_two))

    lax.fori_loop(0, YB, up, (pick(starts[0]), pick(starts[2])), unroll=8)

    below = pick(rows_below)

    def down(step, carry):
        ones, twos, after, here = carry
        y = YB - 1 - step
        slope = first_ref[k * YB + y]
        curve = VISCOSITY * second_ref[k * YB + y]
        bend = VISCOSITY * slope * slope
        factor = curve - slope * here[1]
        new_one, new_two, before_all = [], [], []
        for c in range(COMPS):
            f = here[c]
            prior = jnp.maximum(y - 1, 0)
            before = jnp.where(y > 0, v_ref[at(c, prior), :], below[c])
            run_one = run_ref[0, at(c, y), :]
            run_two = run_ref[1, at(c, y), :]
            eta_one = (ONE.up * ONE.r) * (run_one - ones[c]) + ONE.near * (before - after[c])
            eta_two = (TWO.up * TWO.r) * (run_two + twos[c]) + TWO.near * (before + after[c]) + TWO.mid * f
            y_ref[at(c, y), :] = factor * eta_one + bend * eta_two
            new_one.append(ones[c] * ONE.r + f)
            new_two.append(twos[c] * TWO.r + f)
            before_all.append(before)
        return (tuple(new_one), tuple(new_two), here, tuple(before_all))

    top = tuple(v_ref[(c * YB + YB - 1) * XB : (c * YB + YB) * XB, :] for c in range(COMPS))
    lax.fori_loop(
        0, YB, down, (pick(starts[1]), pick(starts[3]), pick(rows_above), top), unroll=8
    )

    for g in range(ROWS // 8):
        f = [v_ref[plane(64 * g, i), :] for i in range(XB)]
        rows = slice(8 * g, 8 * g + 8)
        ext = [low_ref[rows, :]] + f + [high_ref[rows, :]]
        runs = []
        for line in LINES:
            left, right = [None], [None]
            for i in range(XB - 1):
                left.append(f[i] if i == 0 else left[-1] * line.r + f[i])
                right.append(f[XB - 1 - i] if i == 0 else right[-1] * line.r + f[XB - 1 - i])
            runs.append((left, right[::-1]))
        for i in range(XB):
            pair_one = ONE.near * (ext[i] - ext[i + 2])
            pair_two = (VISCOSITY * TWO.near) * (ext[i] + ext[i + 2]) + (VISCOSITY * TWO.mid) * f[i]
            (left, right), (left_two, right_two) = runs
            for value, sign in ((left[i], 1.0), (right[i], -1.0)):
                if value is not None:
                    pair_one = pair_one + (sign * ONE.up * ONE.r) * value
            for value in (left_two[i], right_two[i]):
                if value is not None:
                    pair_two = pair_two + (VISCOSITY * TWO.up * TWO.r) * value
            u = v_ref[plane(64 * (g % 8), i), :]
            if g < 8:
                u_ref[64 * g + 8 * i : 64 * g + 8 * i + 8, :] = u
            total = y_ref[plane(64 * g, i), :] - u * pair_one + pair_two
            acc_ref[64 * g + 8 * i : 64 * g + 8 * i + 8, :] = total


def finish(acc_ref, u_ref, far_ref, out_ref):
    for g in range(ROWS // 8):
        part, at = divmod(8 * g, PART)
        left_one, right_one, left_two, right_two = (
            far_ref[part, m * PART + at : m * PART + at + 8, :] for m in range(4)
        )
        for i in range(XB):
            one = (ONE.up * ONE.r ** (i + 1)) * left_one - (ONE.up * ONE.r ** (XB - i)) * right_one
            two = (VISCOSITY * TWO.up * TWO.r ** (i + 1)) * left_two
            two = two + (VISCOSITY * TWO.up * TWO.r ** (XB - i)) * right_two
            u = u_ref[64 * (g % 8) + 8 * i : 64 * (g % 8) + 8 * i + 8, :]
            acc = acc_ref[64 * g + 8 * i : 64 * g + 8 * i + 8, :]
            out_ref[plane(64 * g, i), :] = (acc + two) - u * one


VMEM = pl.BlockSpec(memory_space=pltpu.VMEM)
SMEM = pl.BlockSpec(memory_space=pltpu.SMEM)


def call(body, name, ins, outs, cycles, scratch=(), after=()):
    count = len(ins)

    def placed(*refs):
        body(*refs[:count], *refs[count + len(after) :])

    shapes = tuple(jax.ShapeDtypeStruct(s, jnp.float32) for s in outs)
    moved = 4 * sum(math.prod(s) for s in outs)
    kernel = pl.pallas_call(
        placed,
        out_shape=shapes if len(shapes) > 1 else shapes[0],
        in_specs=list(ins) + [pl.BlockSpec(memory_space=pl.ANY)] * len(after),
        out_specs=tuple(VMEM for _ in outs) if len(outs) > 1 else VMEM,
        scratch_shapes=list(scratch),
        name=name,
        compiler_params=pltpu.CompilerParams(vmem_limit_bytes=12 << 20),
        cost_estimate=pl.CostEstimate(flops=cycles * 1024, bytes_accessed=2 * moved, transcendentals=0),
    )
    return lambda *arrays: kernel(*arrays, *after)


def on_device(velocity, metric_first, metric_second):
    px = lax.axis_size("px")
    pz = lax.axis_size("pz")
    groups = px // GROUP
    adjacent = [[GROUP * q + j for j in range(GROUP)] for q in range(groups)]
    across = [[GROUP * q + j for q in range(groups)] for j in range(GROUP)]
    place = jnp.stack([lax.axis_index("px") // GROUP, lax.axis_index("pz")]).astype(jnp.int32)
    ring = jnp.asarray(ring_table(groups, GROUP * XB))
    wall = jnp.asarray(wall_table(pz, YB))
    v = velocity.reshape(ROWS * XB, LANES)

    near = call(moments_x, "moments_x", [VMEM], [(GROUP, 4 * PART, LANES)], 1500)(v)
    near = lax.all_to_all(near, "px", 0, 0, tiled=True, axis_index_groups=adjacent)
    here, low, high = call(
        moments_y,
        "moments_y",
        [SMEM, SMEM, VMEM],
        [(6 * YROWS, LANES)] + [(ROWS, LANES)] * 2,
        1500,
    )(place, wall, v)
    partner = lax.ppermute(here, "pz", [(i, i ^ 1) for i in range(pz)])
    shifts = range(2, pz, 2)
    sent = call(
        pair_up,
        "pair_up",
        [VMEM] * 2,
        [((9 if shift in (2, pz - 2) else 8) * YROWS, LANES) for shift in shifts],
        200,
    )(here, partner)
    far = call(group_moments, "group_moments", [VMEM], [(groups, 4 * PART, LANES)], 300, after=[sent[0]])(near)
    far = lax.all_to_all(far, "px", 0, 0, tiled=True, axis_index_groups=across)

    sides = [here, partner]
    for shift, pair in zip(shifts, sent):
        sides.append(lax.ppermute(pair, "pz", [(i, (i + shift) % pz) for i in range(pz)]))
    from_below = lax.ppermute(high, "px", [(i, (i + 1) % px) for i in range(px)])
    from_above = lax.ppermute(low, "px", [((i + 1) % px, i) for i in range(px)])

    back = call(
        entering,
        "entering",
        [SMEM, SMEM, VMEM, VMEM],
        [(GROUP, 4 * PART, LANES)],
        400,
        after=[from_below, from_above, *sides[2:]],
    )(place, ring, near, far)
    acc, u = call(
        local_terms,
        "local_terms",
        [SMEM] * 4 + [VMEM] * (3 + len(sides)),
        [(ROWS * XB, LANES), (YB * XB, LANES)],
        5000,
        [pltpu.VMEM((2, ROWS * XB, LANES), jnp.float32), pltpu.VMEM((ROWS * XB, LANES), jnp.float32)],
        after=[back],
    )(place, wall, metric_first, metric_second, v, from_below, from_above, *sides)
    back = lax.all_to_all(back, "px", 0, 0, tiled=True, axis_index_groups=adjacent)
    out = call(finish, "finish", [VMEM] * 3, [(ROWS * XB, LANES)], 800)(acc, u, back)
    return out.reshape(velocity.shape)


def solution(mesh):
    return jax.shard_map(
        on_device,
        mesh=mesh,
        in_specs=(P(None, "pz", "px", None), P(), P()),
        out_specs=P(None, "pz", "px", None),
        check_vma=False,
    )
```

```python
import functools
import math

import jax
import jax.numpy as jnp
import numpy as np
from jax import lax
from jax.experimental import pallas as pl
from jax.experimental.pallas import tpu as pltpu
from jax.sharding import PartitionSpec as P


FIRST_ALPHA = 0.4998
FIRST_NEAR = 2.0 * (FIRST_ALPHA + 2.0) / 3.0
FIRST_FAR = (4.0 * FIRST_ALPHA - 1.0) / 3.0
SECOND_ALPHA = 2.0 / 11.0
SECOND_NEAR = 12.0 / 11.0
SECOND_FAR = 3.0 / 11.0
VISCOSITY = 0.5

COMPS = 3
YB = 64
XB = 8
LANES = 128
ROWS = COMPS * YB
GROUP = 8
PART = ROWS // GROUP
YROWS = COMPS * XB


class Line:
    def __init__(self, alpha, stencil, sign):
        root = math.sqrt(1.0 - 4.0 * alpha * alpha)
        self.r = -2.0 * alpha / (1.0 + root)
        green = [self.r ** abs(n) / root for n in range(-4, 5)]
        reply = [sum(stencil[k + 2] * green[n + k + 4] for k in range(-2, 3)) for n in (0, 1, 2)]
        self.sign = sign
        self.mid = reply[0]
        self.up = reply[2] / self.r**2
        self.near = reply[1] - self.up * self.r


ONE = Line(
    FIRST_ALPHA,
    [-FIRST_FAR / 4, -FIRST_NEAR / 2, 0.0, FIRST_NEAR / 2, FIRST_FAR / 4],
    -1.0,
)
TWO = Line(
    SECOND_ALPHA,
    [
        SECOND_FAR / 4,
        SECOND_NEAR,
        -2.0 * SECOND_NEAR - SECOND_FAR / 2,
        SECOND_NEAR,
        SECOND_FAR / 4,
    ],
    1.0,
)
LINES = (ONE, TWO)


def ring_table(groups, cells):
    pairs = groups // 2
    table = np.zeros((groups, 4 * pairs + 16))
    for q in range(groups):
        for s, line in enumerate(LINES):
            sigma = line.r**cells
            for d in range(1, pairs + 1):
                weight = sigma ** (2 * d - 2) / (1.0 - sigma**groups)
                table[q, (2 * s) * pairs + (q // 2 - d) % pairs] += weight
                table[q, (2 * s + 1) * pairs + (q // 2 + d) % pairs] += weight
            up, down = ((1.0, sigma), (sigma, 1.0)) if q % 2 else ((sigma, 1.0), (1.0, sigma))
            low, high = ((1.0, sigma), (0.0, 1.0)) if q % 2 else ((0.0, 1.0), (1.0, sigma))
            table[q, 4 * pairs + 8 * s : 4 * pairs + 8 * s + 8] = (*up, *down, *low, *high)
    return table.astype(np.float32)


def wall_table(blocks, cells):
    stages = blocks.bit_length() - 1
    table = np.zeros((blocks, 18 * stages + 12))
    for k in range(blocks):
        for stage in range(stages):
            size = 1 << stage
            inside = k % size
            below = (k >> stage) & 1
            row = table[k, 18 * stage : 18 * stage + 18]
            for s, line in enumerate(LINES):
                rho = line.r**cells
                own, other = (1.0, rho**size) if below else (rho**size, 1.0)
                row[2 * s : 2 * s + 2] = own, other
                row[6 + 2 * s : 8 + 2 * s] = other, own
                row[12 + 2 * s] = rho**inside if below else 0.0
                row[13 + 2 * s] = 0.0 if below else rho ** (size - 1 - inside)
            row[4:6] = (1.0, 0.0) if below else (0.0, 1.0)
            row[10:12] = (0.0, 1.0) if below else (1.0, 0.0)
            row[16] = float(below and inside == 0)
            row[17] = float(not below and inside == size - 1)
        row = table[k, 18 * stages :]
        for s, line in enumerate(LINES):
            rho = line.r**cells
            eps = line.r ** (blocks * cells + 1)
            up, down = line.up, line.sign * line.up
            scale = -line.r / (1.0 - eps * eps)
            low, high = rho**k / up, rho ** (blocks - 1 - k) / down
            row[4 * s : 4 * s + 4] = (
                -scale * eps * up * low,
                scale * down * low,
                scale * up * high,
                -scale * eps * down * high,
            )
            edge = line.near / (line.up * line.r)
            row[8 + s] = edge if k == 0 else 0.0
            row[10 + s] = edge if k == blocks - 1 else 0.0
    return table.astype(np.float32)


class Chosen:
    def __init__(self, table, index):
        self.table = table
        self.here = [index == j for j in range(1, len(table))]

    def __getitem__(self, m):
        value = float(self.table[0, m])
        for here, entry in zip(self.here, self.table[1:, m]):
            value = jnp.where(here, float(entry), value)
        return value


def plane(base, index):
    return pl.ds(base + index, 8, stride=XB)


def top_half(shape):
    return lax.broadcasted_iota(jnp.int32, shape, 0) % 8 < 4


def by_line(rows, one, two):
    return jnp.where(top_half((rows, LANES)), one, two)


def moments_x(v_hbm, out_hbm, v_ref, out_ref, in_sems, out_sems):
    def fetch(part):
        rows = pl.ds(part * PART * XB, PART * XB)
        return pltpu.make_async_copy(v_hbm.at[rows], v_ref.at[rows], in_sems.at[part])

    def send(part):
        return pltpu.make_async_copy(out_ref.at[part], out_hbm.at[part], out_sems.at[part])

    for part in range(GROUP):
        fetch(part).start()
    for part in range(GROUP):
        fetch(part).wait()
        for g in range(part * PART // 8, (part + 1) * PART // 8):
            sums = [None] * 4
            for i in range(XB):
                f = v_ref[plane(64 * g, i), :]
                for s, line in enumerate(LINES):
                    sums[2 * s] = f if i == 0 else sums[2 * s] * line.r + f
                    sums[2 * s + 1] = f if i == 0 else sums[2 * s + 1] + line.r**i * f
            for side in range(2):
                one, two = sums[side], sums[2 + side]
                tiles = (by_line(8, one, pltpu.roll(two, 4, 0)), by_line(8, pltpu.roll(one, 4, 0), two))
                for half in range(2):
                    at = 2 * PART * side + 2 * (8 * g + 4 * half - part * PART)
                    out_ref[part, at : at + 8, :] = tiles[half]
        send(part).start()
    for part in range(GROUP):
        send(part).wait()


def moments_y(place_ref, table_ref, v_ref, here_ref, low_ref, high_ref):
    k = place_ref[1]
    base = table_ref.shape[1] - 4
    for c in range(COMPS):
        sums = [None] * 4
        first = v_ref[c * YB * XB : c * YB * XB + XB, :]
        for y in range(YB):
            f = v_ref[(c * YB + y) * XB : (c * YB + y + 1) * XB, :]
            for s, line in enumerate(LINES):
                sums[2 * s] = f if y == 0 else sums[2 * s] * line.r + f
                sums[2 * s + 1] = f if y == 0 else sums[2 * s + 1] + line.r**y * f
        last = f
        for s in range(2):
            sums[2 * s] = sums[2 * s] + table_ref[k, base + 2 + s] * last
            sums[2 * s + 1] = sums[2 * s + 1] + table_ref[k, base + s] * first
        for m, value in enumerate((*sums, last, first)):
            here_ref[m * YROWS + c * XB : m * YROWS + (c + 1) * XB, :] = value
    for g in range(ROWS // 8):
        low_ref[8 * g : 8 * g + 8, :] = v_ref[plane(64 * g, 0), :]
        high_ref[8 * g : 8 * g + 8, :] = v_ref[plane(64 * g, XB - 1), :]


def values(ref, m):
    return ref[m * YROWS : (m + 1) * YROWS, :]


def entered(stage, weights, sibling_ref, so_far):
    terms = [weights[18 * stage + 12 + m] * values(sibling_ref, m) for m in range(6)]
    return terms if so_far is None else [value + term for value, term in zip(so_far, terms)]


def joined(stage, weights, cube_ref, sibling_ref):
    at = 18 * stage
    return [
        weights[at + m] * values(cube_ref, m) + weights[at + 6 + m] * values(sibling_ref, m) for m in range(6)
    ]


def join(stage, table, cube_ref, sibling_ref, *refs):
    weights = Chosen(table, lax.axis_index("pz"))
    *before, cube_out, entering_out = refs
    so_far = [values(before[0], m) for m in range(6)] if before else None
    for m, value in enumerate(joined(stage, weights, cube_ref, sibling_ref)):
        cube_out[m * YROWS : (m + 1) * YROWS, :] = value
    for m, value in enumerate(entered(stage, weights, sibling_ref, so_far)):
        entering_out[m * YROWS : (m + 1) * YROWS, :] = value


def group_moments(near_ref, out_ref):
    rho = by_line(2 * PART, ONE.r**XB, TWO.r**XB)
    up = near_ref[0, 0 : 2 * PART, :]
    down = near_ref[GROUP - 1, 2 * PART : 4 * PART, :]
    for j in range(1, GROUP):
        up = up * rho + near_ref[j, 0 : 2 * PART, :]
        down = down * rho + near_ref[GROUP - 1 - j, 2 * PART : 4 * PART, :]
    out_ref[0 : 2 * PART, :] = up
    out_ref[2 * PART : 4 * PART, :] = down


def pair_weight(weights, m):
    at = weights.table.shape[1] - 16 + m
    return by_line(2 * PART, weights[at], weights[at + 8])


def pair_moments(table, own_ref, sibling_ref, out_hbm, out_ref, sems):
    weights = Chosen(table, lax.axis_index("px") // GROUP)
    for side in range(2):
        rows = slice(2 * PART * side, 2 * PART * (side + 1))
        total = pair_weight(weights, 2 * side) * own_ref[rows, :]
        out_ref[rows, :] = total + pair_weight(weights, 2 * side + 1) * sibling_ref[rows, :]
    copies = [pltpu.make_async_copy(out_ref, out_hbm.at[j], sems.at[j]) for j in range(out_hbm.shape[0])]
    for copy in copies:
        copy.start()
    for copy in copies:
        copy.wait()


def entering(table, near_ref, sibling_ref, far_ref, out_hbm, out_ref, sems):
    weights = Chosen(table, lax.axis_index("px") // GROUP)
    pairs = far_ref.shape[0]
    rho = by_line(2 * PART, ONE.r**XB, TWO.r**XB)
    copies = [pltpu.make_async_copy(out_ref.at[j], out_hbm.at[j], sems.at[j]) for j in range(GROUP)]
    for side in range(2):
        rows = slice(2 * PART * side, 2 * PART * (side + 1))
        total = None
        for j in range(pairs):
            weight = by_line(2 * PART, weights[side * pairs + j], weights[(2 + side) * pairs + j])
            term = weight * far_ref[j, rows, :]
            total = term if total is None else total + term
        total = pair_weight(weights, 5 + 2 * side) * total
        total = total + pair_weight(weights, 4 + 2 * side) * sibling_ref[rows, :]
        for j in range(GROUP):
            here = j if side == 0 else GROUP - 1 - j
            out_ref[here, rows, :] = total
            if side == 1:
                copies[here].start()
            if j < GROUP - 1:
                total = total * rho + near_ref[here, rows, :]
    for copy in copies:
        copy.wait()


def local_terms(
    last, place_ref, table_ref, first_ref, second_ref, v_ref, low_ref, high_ref, cube_ref, sibling_ref, before_ref,
    acc_ref, u_ref, run_ref, y_ref,
):
    k = place_ref[1]
    so_far = [values(before_ref, m) for m in range(6)]
    weights = [table_ref[k, m] for m in range(table_ref.shape[1])]
    whole = joined(last, weights, cube_ref, sibling_ref)
    *starts, rows_below, rows_above = entered(last, weights, sibling_ref, so_far)
    for s in range(2):
        for side in range(2):
            for sign in range(2):
                weight = table_ref[k, 18 * (last + 1) + 4 * s + 2 * side + sign]
                starts[2 * s + side] = starts[2 * s + side] + weight * whole[2 * s + sign]

    def pick(total):
        return tuple(total[c * XB : (c + 1) * XB] for c in range(COMPS))

    def at(c, y):
        return pl.ds(pl.multiple_of((c * YB + y) * XB, XB), XB)

    def up(y, carry):
        ones, twos = carry
        new_one, new_two = [], []
        for c in range(COMPS):
            run_ref[0, at(c, y), :] = ones[c]
            run_ref[1, at(c, y), :] = twos[c]
            f = v_ref[at(c, y), :]
            new_one.append(ones[c] * ONE.r + f)
            new_two.append(twos[c] * TWO.r + f)
        return (tuple(new_one), tuple(new_two))

    lax.fori_loop(0, YB, up, (pick(starts[0]), pick(starts[2])), unroll=8)

    below = pick(rows_below)

    def down(step, carry):
        ones, twos, after, here = carry
        y = YB - 1 - step
        slope = first_ref[k * YB + y]
        curve = VISCOSITY * second_ref[k * YB + y]
        bend = VISCOSITY * slope * slope
        factor = curve - slope * here[1]
        new_one, new_two, before_all = [], [], []
        for c in range(COMPS):
            f = here[c]
            prior = jnp.maximum(y - 1, 0)
            before = jnp.where(y > 0, v_ref[at(c, prior), :], below[c])
            run_one = run_ref[0, at(c, y), :]
            run_two = run_ref[1, at(c, y), :]
            eta_one = (ONE.up * ONE.r) * (run_one - ones[c]) + ONE.near * (before - after[c])
            eta_two = (TWO.up * TWO.r) * (run_two + twos[c]) + TWO.near * (before + after[c]) + TWO.mid * f
            y_ref[at(c, y), :] = factor * eta_one + bend * eta_two
            new_one.append(ones[c] * ONE.r + f)
            new_two.append(twos[c] * TWO.r + f)
            before_all.append(before)
        return (tuple(new_one), tuple(new_two), here, tuple(before_all))

    top = tuple(v_ref[(c * YB + YB - 1) * XB : (c * YB + YB) * XB, :] for c in range(COMPS))
    lax.fori_loop(
        0, YB, down, (pick(starts[1]), pick(starts[3]), pick(rows_above), top), unroll=8
    )

    for g in range(ROWS // 8):
        f = [v_ref[plane(64 * g, i), :] for i in range(XB)]
        rows = slice(8 * g, 8 * g + 8)
        ext = [low_ref[rows, :]] + f + [high_ref[rows, :]]
        runs = []
        for line in LINES:
            left, right = [None], [None]
            for i in range(XB - 1):
                left.append(f[i] if i == 0 else left[-1] * line.r + f[i])
                right.append(f[XB - 1 - i] if i == 0 else right[-1] * line.r + f[XB - 1 - i])
            runs.append((left, right[::-1]))
        for i in range(XB):
            pair_one = ONE.near * (ext[i] - ext[i + 2])
            pair_two = (VISCOSITY * TWO.near) * (ext[i] + ext[i + 2]) + (VISCOSITY * TWO.mid) * f[i]
            (left, right), (left_two, right_two) = runs
            for value, sign in ((left[i], 1.0), (right[i], -1.0)):
                if value is not None:
                    pair_one = pair_one + (sign * ONE.up * ONE.r) * value
            for value in (left_two[i], right_two[i]):
                if value is not None:
                    pair_two = pair_two + (VISCOSITY * TWO.up * TWO.r) * value
            u = v_ref[plane(64 * (g % 8), i), :]
            if g < 8:
                u_ref[64 * g + 8 * i : 64 * g + 8 * i + 8, :] = u
            total = y_ref[plane(64 * g, i), :] - u * pair_one + pair_two
            acc_ref[64 * g + 8 * i : 64 * g + 8 * i + 8, :] = total


def finish(acc_ref, u_ref, far_ref, out_hbm, out_ref, sems):
    def send(part):
        rows = pl.ds(part * PART * XB, PART * XB)
        return pltpu.make_async_copy(out_ref.at[rows], out_hbm.at[rows], sems.at[part])

    for g in range(ROWS // 8):
        sums = []
        for side in range(2):
            tiles = []
            for half in range(2):
                part, at = divmod(8 * g + 4 * half, PART)
                at = 2 * PART * side + 2 * at
                tiles.append(far_ref[part, at : at + 8, :])
            sums.append(by_line(8, tiles[0], pltpu.roll(tiles[1], 4, 0)))
            sums.append(by_line(8, pltpu.roll(tiles[0], 4, 0), tiles[1]))
        left_one, left_two, right_one, right_two = sums
        for i in range(XB):
            one = (ONE.up * ONE.r ** (i + 1)) * left_one - (ONE.up * ONE.r ** (XB - i)) * right_one
            two = (VISCOSITY * TWO.up * TWO.r ** (i + 1)) * left_two
            two = two + (VISCOSITY * TWO.up * TWO.r ** (XB - i)) * right_two
            u = u_ref[64 * (g % 8) + 8 * i : 64 * (g % 8) + 8 * i + 8, :]
            acc = acc_ref[64 * g + 8 * i : 64 * g + 8 * i + 8, :]
            out_ref[plane(64 * g, i), :] = (acc + two) - u * one
        if 8 * (g + 1) % PART == 0:
            send(8 * g // PART).start()
    for part in range(GROUP):
        send(part).wait()


VMEM = pl.BlockSpec(memory_space=pltpu.VMEM)
SMEM = pl.BlockSpec(memory_space=pltpu.SMEM)
ANY = pl.BlockSpec(memory_space=pl.ANY)


def staged(shape, *counts):
    return [pltpu.VMEM(shape, jnp.float32)] + [pltpu.SemaphoreType.DMA((n,)) for n in counts]


def call(body, ins, outs, cycles, scratch=(), after=(), to=None, vmem=12):
    count = len(ins)

    def placed(*refs):
        body(*refs[:count], *refs[count + len(after) :])

    shapes = tuple(jax.ShapeDtypeStruct(s, jnp.float32) for s in outs)
    moved = 4 * sum(math.prod(s) for s in outs)
    kernel = pl.pallas_call(
        placed,
        out_shape=shapes if len(shapes) > 1 else shapes[0],
        in_specs=list(ins) + [pl.BlockSpec(memory_space=pl.ANY)] * len(after),
        out_specs=tuple(to or VMEM for _ in outs) if len(outs) > 1 else to or VMEM,
        scratch_shapes=list(scratch),
        compiler_params=pltpu.CompilerParams(vmem_limit_bytes=vmem << 20),
        cost_estimate=pl.CostEstimate(flops=cycles * 1024, bytes_accessed=2 * moved, transcendentals=0),
    )

    def run(*arrays):
        return kernel(*arrays, *after)

    return run


def on_device(velocity, metric_first, metric_second):
    px = lax.axis_size("px")
    pz = lax.axis_size("pz")
    groups = px // GROUP
    adjacent = [[GROUP * q + j for j in range(GROUP)] for q in range(groups)]
    across = [[j + 2 * GROUP * q for q in range(groups // 2)] for j in range(2 * GROUP)]
    place = jnp.stack([lax.axis_index("px") // GROUP, lax.axis_index("pz")]).astype(jnp.int32)
    ring = ring_table(groups, GROUP * XB)
    wall_rows = wall_table(pz, YB)
    wall = jnp.asarray(wall_rows)
    chunk = (GROUP, 4 * PART, LANES)
    v = velocity.reshape(ROWS * XB, LANES)

    whole = (ROWS * XB, LANES)
    scratch = [pltpu.VMEM(whole, jnp.float32)] + staged(chunk, GROUP, GROUP)
    near = call(moments_x, [ANY], [chunk], 1500, scratch, to=ANY, vmem=60)(v)
    near = lax.all_to_all(near, "px", 0, 0, tiled=True, axis_index_groups=adjacent)
    here, low, high = call(
        moments_y, [SMEM, SMEM, VMEM], [(6 * YROWS, LANES)] + [(ROWS, LANES)] * 2, 1500
    )(place, wall, v)

    def sibling_of(cube, stage):
        return lax.ppermute(cube, "pz", [(i, i ^ (1 << stage)) for i in range(pz)])

    def join_stage(stage, *arrays):
        body = functools.partial(join, stage, wall_rows)
        cube = [(6 * YROWS, LANES)] * 2
        return call(body, [VMEM] * len(arrays), cube, 200)(*arrays)

    stages = pz.bit_length() - 1
    sibling = sibling_of(here, 0)
    cube, inflow = join_stage(0, here, sibling)
    own = call(group_moments, [VMEM], [(4 * PART, LANES)], 300, after=[cube])(near)
    other = lax.ppermute(own, "px", [(i, i ^ GROUP) for i in range(px)])
    pair_chunk = (groups // 2, 4 * PART, LANES)
    far = call(
        functools.partial(pair_moments, ring),
        [VMEM] * 2,
        [pair_chunk],
        300,
        staged(pair_chunk[1:], groups // 2),
        to=ANY,
    )(own, other)
    far = lax.all_to_all(far, "px", 0, 0, tiled=True, axis_index_groups=across)

    for stage in range(1, stages):
        sibling = sibling_of(cube, stage)
        if stage < stages - 1:
            cube, inflow = join_stage(stage, cube, sibling, inflow)
    from_below = lax.ppermute(high, "px", [(i, (i + 1) % px) for i in range(px)])
    from_above = lax.ppermute(low, "px", [((i + 1) % px, i) for i in range(px)])

    back = call(
        functools.partial(entering, ring),
        [VMEM] * 3,
        [chunk],
        400,
        staged(chunk, GROUP),
        after=[from_below, from_above],
        to=ANY,
    )(near, other, far)
    acc, u = call(
        functools.partial(local_terms, stages - 1),
        [SMEM] * 4 + [VMEM] * 6,
        [(ROWS * XB, LANES), (YB * XB, LANES)],
        5000,
        [pltpu.VMEM((2, ROWS * XB, LANES), jnp.float32), pltpu.VMEM((ROWS * XB, LANES), jnp.float32)],
        after=[back],
    )(place, wall, metric_first, metric_second, v, from_below, from_above, cube, sibling, inflow)
    back = lax.all_to_all(back, "px", 0, 0, tiled=True, axis_index_groups=adjacent)
    out = call(finish, [VMEM] * 3, [whole], 800, staged(whole, GROUP), to=ANY)(acc, u, back)
    return out.reshape(velocity.shape)


def solution(mesh):
    return jax.shard_map(
        on_device,
        mesh=mesh,
        in_specs=(P(None, "pz", "px", None), P(), P()),
        out_specs=P(None, "pz", "px", None),
        check_vma=False,
    )
```

```python
import functools
import math

import jax
import jax.numpy as jnp
import numpy as np
from jax import lax
from jax.experimental import pallas as pl
from jax.experimental.pallas import tpu as pltpu
from jax.sharding import PartitionSpec as P


FIRST_ALPHA = 0.4998
FIRST_NEAR = 2.0 * (FIRST_ALPHA + 2.0) / 3.0
FIRST_FAR = (4.0 * FIRST_ALPHA - 1.0) / 3.0
SECOND_ALPHA = 2.0 / 11.0
SECOND_NEAR = 12.0 / 11.0
SECOND_FAR = 3.0 / 11.0
VISCOSITY = 0.5

COMPS = 3
YB = 64
XB = 8
LANES = 128
ROWS = COMPS * YB
GROUP = 8
PART = ROWS // GROUP
YROWS = COMPS * XB


class Line:
    def __init__(self, alpha, stencil, sign):
        root = math.sqrt(1.0 - 4.0 * alpha * alpha)
        self.r = -2.0 * alpha / (1.0 + root)
        green = [self.r ** abs(n) / root for n in range(-4, 5)]
        reply = [sum(stencil[k + 2] * green[n + k + 4] for k in range(-2, 3)) for n in (0, 1, 2)]
        self.sign = sign
        self.mid = reply[0]
        self.up = reply[2] / self.r**2
        self.near = reply[1] - self.up * self.r


ONE = Line(
    FIRST_ALPHA,
    [-FIRST_FAR / 4, -FIRST_NEAR / 2, 0.0, FIRST_NEAR / 2, FIRST_FAR / 4],
    -1.0,
)
TWO = Line(
    SECOND_ALPHA,
    [
        SECOND_FAR / 4,
        SECOND_NEAR,
        -2.0 * SECOND_NEAR - SECOND_FAR / 2,
        SECOND_NEAR,
        SECOND_FAR / 4,
    ],
    1.0,
)
LINES = (ONE, TWO)


def ring_table(groups, cells):
    pairs = groups // 2
    table = np.zeros((groups, 4 * pairs + 16))
    for q in range(groups):
        for s, line in enumerate(LINES):
            sigma = line.r**cells
            for d in range(1, pairs + 1):
                weight = sigma ** (2 * d - 2) / (1.0 - sigma**groups)
                table[q, (2 * s) * pairs + (q // 2 - d) % pairs] += weight
                table[q, (2 * s + 1) * pairs + (q // 2 + d) % pairs] += weight
            up, down = ((1.0, sigma), (sigma, 1.0)) if q % 2 else ((sigma, 1.0), (1.0, sigma))
            low, high = ((1.0, sigma), (0.0, 1.0)) if q % 2 else ((0.0, 1.0), (1.0, sigma))
            table[q, 4 * pairs + 8 * s : 4 * pairs + 8 * s + 8] = (*up, *down, *low, *high)
    return table.astype(np.float32)


def wall_table(blocks, cells):
    stages = blocks.bit_length() - 1
    table = np.zeros((blocks, 18 * stages + 12))
    for k in range(blocks):
        for stage in range(stages):
            size = 1 << stage
            inside = k % size
            below = (k >> stage) & 1
            row = table[k, 18 * stage : 18 * stage + 18]
            for s, line in enumerate(LINES):
                rho = line.r**cells
                own, other = (1.0, rho**size) if below else (rho**size, 1.0)
                row[2 * s : 2 * s + 2] = own, other
                row[6 + 2 * s : 8 + 2 * s] = other, own
                row[12 + 2 * s] = rho**inside if below else 0.0
                row[13 + 2 * s] = 0.0 if below else rho ** (size - 1 - inside)
            row[4:6] = (1.0, 0.0) if below else (0.0, 1.0)
            row[10:12] = (0.0, 1.0) if below else (1.0, 0.0)
            row[16] = float(below and inside == 0)
            row[17] = float(not below and inside == size - 1)
        row = table[k, 18 * stages :]
        for s, line in enumerate(LINES):
            rho = line.r**cells
            eps = line.r ** (blocks * cells + 1)
            up, down = line.up, line.sign * line.up
            scale = -line.r / (1.0 - eps * eps)
            low, high = rho**k / up, rho ** (blocks - 1 - k) / down
            row[4 * s : 4 * s + 4] = (
                -scale * eps * up * low,
                scale * down * low,
                scale * up * high,
                -scale * eps * down * high,
            )
            edge = line.near / (line.up * line.r)
            row[8 + s] = edge if k == 0 else 0.0
            row[10 + s] = edge if k == blocks - 1 else 0.0
    return table.astype(np.float32)


class Chosen:
    def __init__(self, table, index):
        self.table = table
        self.here = [index == j for j in range(1, len(table))]

    def __getitem__(self, m):
        value = float(self.table[0, m])
        for here, entry in zip(self.here, self.table[1:, m]):
            value = jnp.where(here, float(entry), value)
        return value


def plane(base, index):
    return pl.ds(base + index, 8, stride=XB)


def top_half(shape):
    return lax.broadcasted_iota(jnp.int32, shape, 0) % 8 < 4


def by_line(rows, one, two):
    return jnp.where(top_half((rows, LANES)), one, two)


def moments_x(v_hbm, out_hbm, v_ref, out_ref, in_sems, out_sems):
    def fetch(part):
        rows = pl.ds(part * PART * XB, PART * XB)
        return pltpu.make_async_copy(v_hbm.at[rows], v_ref.at[rows], in_sems.at[part])

    def send(part):
        return pltpu.make_async_copy(out_ref.at[part], out_hbm.at[part], out_sems.at[part])

    for part in range(GROUP):
        fetch(part).start()
    for part in range(GROUP):
        fetch(part).wait()
        for g in range(part * PART // 8, (part + 1) * PART // 8):
            sums = [None] * 4
            for i in range(XB):
                f = v_ref[plane(64 * g, i), :]
                for s, line in enumerate(LINES):
                    sums[2 * s] = f if i == 0 else sums[2 * s] * line.r + f
                    sums[2 * s + 1] = f if i == 0 else sums[2 * s + 1] + line.r**i * f
            for side in range(2):
                one, two = sums[side], sums[2 + side]
                tiles = (by_line(8, one, pltpu.roll(two, 4, 0)), by_line(8, pltpu.roll(one, 4, 0), two))
                for half in range(2):
                    at = 2 * PART * side + 2 * (8 * g + 4 * half - part * PART)
                    out_ref[part, at : at + 8, :] = tiles[half]
        send(part).start()
    for part in range(GROUP):
        send(part).wait()


def moments_y(place_ref, table_ref, v_ref, here_ref, low_ref, high_ref):
    k = place_ref[1]
    base = table_ref.shape[1] - 4
    for c in range(COMPS):
        sums = [None] * 4
        first = v_ref[c * YB * XB : c * YB * XB + XB, :]
        for y in range(YB):
            f = v_ref[(c * YB + y) * XB : (c * YB + y + 1) * XB, :]
            for s, line in enumerate(LINES):
                sums[2 * s] = f if y == 0 else sums[2 * s] * line.r + f
                sums[2 * s + 1] = f if y == 0 else sums[2 * s + 1] + line.r**y * f
        last = f
        for s in range(2):
            sums[2 * s] = sums[2 * s] + table_ref[k, base + 2 + s] * last
            sums[2 * s + 1] = sums[2 * s + 1] + table_ref[k, base + s] * first
        for m, value in enumerate((*sums, last, first)):
            here_ref[m * YROWS + c * XB : m * YROWS + (c + 1) * XB, :] = value
    for g in range(ROWS // 8):
        low_ref[8 * g : 8 * g + 8, :] = v_ref[plane(64 * g, 0), :]
        high_ref[8 * g : 8 * g + 8, :] = v_ref[plane(64 * g, XB - 1), :]


def values(ref, m):
    return ref[m * YROWS : (m + 1) * YROWS, :]


def entered(stage, weights, sibling_ref, so_far):
    terms = [weights[18 * stage + 12 + m] * values(sibling_ref, m) for m in range(6)]
    return terms if so_far is None else [value + term for value, term in zip(so_far, terms)]


def joined(stage, weights, cube_ref, sibling_ref):
    at = 18 * stage
    return [
        weights[at + m] * values(cube_ref, m) + weights[at + 6 + m] * values(sibling_ref, m) for m in range(6)
    ]


def join(stage, table, cube_ref, sibling_ref, *refs):
    weights = Chosen(table, lax.axis_index("pz"))
    *before, cube_out, entering_out = refs
    so_far = [values(before[0], m) for m in range(6)] if before else None
    for m, value in enumerate(joined(stage, weights, cube_ref, sibling_ref)):
        cube_out[m * YROWS : (m + 1) * YROWS, :] = value
    for m, value in enumerate(entered(stage, weights, sibling_ref, so_far)):
        entering_out[m * YROWS : (m + 1) * YROWS, :] = value


def group_moments(near_ref, out_ref):
    rho = by_line(2 * PART, ONE.r**XB, TWO.r**XB)
    up = near_ref[0, 0 : 2 * PART, :]
    down = near_ref[GROUP - 1, 2 * PART : 4 * PART, :]
    for j in range(1, GROUP):
        up = up * rho + near_ref[j, 0 : 2 * PART, :]
        down = down * rho + near_ref[GROUP - 1 - j, 2 * PART : 4 * PART, :]
    out_ref[0 : 2 * PART, :] = up
    out_ref[2 * PART : 4 * PART, :] = down


def pair_weight(weights, m):
    at = weights.table.shape[1] - 16 + m
    return by_line(2 * PART, weights[at], weights[at + 8])


def pair_moments(table, own_ref, sibling_ref, out_hbm, out_ref, sems):
    weights = Chosen(table, lax.axis_index("px") // GROUP)
    for side in range(2):
        rows = slice(2 * PART * side, 2 * PART * (side + 1))
        total = pair_weight(weights, 2 * side) * own_ref[rows, :]
        out_ref[rows, :] = total + pair_weight(weights, 2 * side + 1) * sibling_ref[rows, :]
    copies = [pltpu.make_async_copy(out_ref, out_hbm.at[j], sems.at[j]) for j in range(out_hbm.shape[0])]
    for copy in copies:
        copy.start()
    for copy in copies:
        copy.wait()


def entering(table, near_ref, sibling_ref, far_ref, out_hbm, out_ref, sems):
    weights = Chosen(table, lax.axis_index("px") // GROUP)
    pairs = far_ref.shape[0]
    rho = by_line(2 * PART, ONE.r**XB, TWO.r**XB)
    copies = [pltpu.make_async_copy(out_ref.at[j], out_hbm.at[j], sems.at[j]) for j in range(GROUP)]
    for side in range(2):
        rows = slice(2 * PART * side, 2 * PART * (side + 1))
        total = None
        for j in range(pairs):
            weight = by_line(2 * PART, weights[side * pairs + j], weights[(2 + side) * pairs + j])
            term = weight * far_ref[j, rows, :]
            total = term if total is None else total + term
        total = pair_weight(weights, 5 + 2 * side) * total
        total = total + pair_weight(weights, 4 + 2 * side) * sibling_ref[rows, :]
        for j in range(GROUP):
            here = j if side == 0 else GROUP - 1 - j
            out_ref[here, rows, :] = total
            if side == 1:
                copies[here].start()
            if j < GROUP - 1:
                total = total * rho + near_ref[here, rows, :]
    for copy in copies:
        copy.wait()


def local_terms(
    last, place_ref, table_ref, first_ref, second_ref, v_ref, low_ref, high_ref, cube_ref, sibling_ref, before_ref,
    acc_ref, u_ref, run_ref, y_ref,
):
    k = place_ref[1]
    so_far = [values(before_ref, m) for m in range(6)]
    weights = [table_ref[k, m] for m in range(table_ref.shape[1])]
    whole = joined(last, weights, cube_ref, sibling_ref)
    *starts, rows_below, rows_above = entered(last, weights, sibling_ref, so_far)
    for s in range(2):
        for side in range(2):
            for sign in range(2):
                weight = table_ref[k, 18 * (last + 1) + 4 * s + 2 * side + sign]
                starts[2 * s + side] = starts[2 * s + side] + weight * whole[2 * s + sign]

    def pick(total):
        return tuple(total[c * XB : (c + 1) * XB] for c in range(COMPS))

    def at(c, y):
        return pl.ds(pl.multiple_of((c * YB + y) * XB, XB), XB)

    def up(y, carry):
        ones, twos = carry
        new_one, new_two = [], []
        for c in range(COMPS):
            run_ref[0, at(c, y), :] = ones[c]
            run_ref[1, at(c, y), :] = twos[c]
            f = v_ref[at(c, y), :]
            new_one.append(ones[c] * ONE.r + f)
            new_two.append(twos[c] * TWO.r + f)
        return (tuple(new_one), tuple(new_two))

    lax.fori_loop(0, YB, up, (pick(starts[0]), pick(starts[2])), unroll=8)

    below = pick(rows_below)

    def down(step, carry):
        ones, twos, after, here = carry
        y = YB - 1 - step
        slope = first_ref[k * YB + y]
        curve = VISCOSITY * second_ref[k * YB + y]
        bend = VISCOSITY * slope * slope
        factor = curve - slope * here[1]
        new_one, new_two, before_all = [], [], []
        for c in range(COMPS):
            f = here[c]
            prior = jnp.maximum(y - 1, 0)
            before = jnp.where(y > 0, v_ref[at(c, prior), :], below[c])
            run_one = run_ref[0, at(c, y), :]
            run_two = run_ref[1, at(c, y), :]
            eta_one = (ONE.up * ONE.r) * (run_one - ones[c]) + ONE.near * (before - after[c])
            eta_two = (TWO.up * TWO.r) * (run_two + twos[c]) + TWO.near * (before + after[c]) + TWO.mid * f
            y_ref[at(c, y), :] = factor * eta_one + bend * eta_two
            new_one.append(ones[c] * ONE.r + f)
            new_two.append(twos[c] * TWO.r + f)
            before_all.append(before)
        return (tuple(new_one), tuple(new_two), here, tuple(before_all))

    top = tuple(v_ref[(c * YB + YB - 1) * XB : (c * YB + YB) * XB, :] for c in range(COMPS))
    lax.fori_loop(
        0, YB, down, (pick(starts[1]), pick(starts[3]), pick(rows_above), top), unroll=8
    )

    for g in range(ROWS // 8):
        f = [v_ref[plane(64 * g, i), :] for i in range(XB)]
        rows = slice(8 * g, 8 * g + 8)
        ext = [low_ref[rows, :]] + f + [high_ref[rows, :]]
        runs = []
        for line in LINES:
            left, right = [None], [None]
            for i in range(XB - 1):
                left.append(f[i] if i == 0 else left[-1] * line.r + f[i])
                right.append(f[XB - 1 - i] if i == 0 else right[-1] * line.r + f[XB - 1 - i])
            runs.append((left, right[::-1]))
        for i in range(XB):
            pair_one = ONE.near * (ext[i] - ext[i + 2])
            pair_two = (VISCOSITY * TWO.near) * (ext[i] + ext[i + 2]) + (VISCOSITY * TWO.mid) * f[i]
            (left, right), (left_two, right_two) = runs
            for value, sign in ((left[i], 1.0), (right[i], -1.0)):
                if value is not None:
                    pair_one = pair_one + (sign * ONE.up * ONE.r) * value
            for value in (left_two[i], right_two[i]):
                if value is not None:
                    pair_two = pair_two + (VISCOSITY * TWO.up * TWO.r) * value
            u = v_ref[plane(64 * (g % 8), i), :]
            if g < 8:
                u_ref[64 * g + 8 * i : 64 * g + 8 * i + 8, :] = u
            total = y_ref[plane(64 * g, i), :] - u * pair_one + pair_two
            acc_ref[64 * g + 8 * i : 64 * g + 8 * i + 8, :] = total


def finish(acc_ref, u_ref, far_ref, out_hbm, out_ref, sems):
    def send(part):
        rows = pl.ds(part * PART * XB, PART * XB)
        return pltpu.make_async_copy(out_ref.at[rows], out_hbm.at[rows], sems.at[part])

    for g in range(ROWS // 8):
        sums = []
        for side in range(2):
            tiles = []
            for half in range(2):
                part, at = divmod(8 * g + 4 * half, PART)
                at = 2 * PART * side + 2 * at
                tiles.append(far_ref[part, at : at + 8, :])
            sums.append(by_line(8, tiles[0], pltpu.roll(tiles[1], 4, 0)))
            sums.append(by_line(8, pltpu.roll(tiles[0], 4, 0), tiles[1]))
        left_one, left_two, right_one, right_two = sums
        for i in range(XB):
            one = (ONE.up * ONE.r ** (i + 1)) * left_one - (ONE.up * ONE.r ** (XB - i)) * right_one
            two = (VISCOSITY * TWO.up * TWO.r ** (i + 1)) * left_two
            two = two + (VISCOSITY * TWO.up * TWO.r ** (XB - i)) * right_two
            u = u_ref[64 * (g % 8) + 8 * i : 64 * (g % 8) + 8 * i + 8, :]
            acc = acc_ref[64 * g + 8 * i : 64 * g + 8 * i + 8, :]
            out_ref[plane(64 * g, i), :] = (acc + two) - u * one
        if 8 * (g + 1) % PART == 0:
            send(8 * g // PART).start()
    for part in range(GROUP):
        send(part).wait()


VMEM = pl.BlockSpec(memory_space=pltpu.VMEM)
SMEM = pl.BlockSpec(memory_space=pltpu.SMEM)
ANY = pl.BlockSpec(memory_space=pl.ANY)


def staged(shape, *counts):
    return [pltpu.VMEM(shape, jnp.float32)] + [pltpu.SemaphoreType.DMA((n,)) for n in counts]


def call(body, ins, outs, cycles, scratch=(), after=(), to=None, vmem=12):
    count = len(ins)

    def placed(*refs):
        body(*refs[:count], *refs[count + len(after) :])

    shapes = tuple(jax.ShapeDtypeStruct(s, jnp.float32) for s in outs)
    moved = 4 * sum(math.prod(s) for s in outs)
    kernel = pl.pallas_call(
        placed,
        out_shape=shapes if len(shapes) > 1 else shapes[0],
        in_specs=list(ins) + [pl.BlockSpec(memory_space=pl.ANY)] * len(after),
        out_specs=tuple(to or VMEM for _ in outs) if len(outs) > 1 else to or VMEM,
        scratch_shapes=list(scratch),
        compiler_params=pltpu.CompilerParams(vmem_limit_bytes=vmem << 20),
        cost_estimate=pl.CostEstimate(flops=cycles * 1024, bytes_accessed=2 * moved, transcendentals=0),
    )

    def run(*arrays):
        return kernel(*arrays, *after)

    return run


def on_device(velocity, metric_first, metric_second):
    px = lax.axis_size("px")
    pz = lax.axis_size("pz")
    groups = px // GROUP
    adjacent = [[GROUP * q + j for j in range(GROUP)] for q in range(groups)]
    across = [[j + 2 * GROUP * q for q in range(groups // 2)] for j in range(2 * GROUP)]
    place = jnp.stack([lax.axis_index("px") // GROUP, lax.axis_index("pz")]).astype(jnp.int32)
    ring = ring_table(groups, GROUP * XB)
    wall_rows = wall_table(pz, YB)
    wall = jnp.asarray(wall_rows)
    chunk = (GROUP, 4 * PART, LANES)
    v = velocity.reshape(ROWS * XB, LANES)

    whole = (ROWS * XB, LANES)
    scratch = [pltpu.VMEM(whole, jnp.float32)] + staged(chunk, GROUP, GROUP)
    near = call(moments_x, [ANY], [chunk], 1500, scratch, to=ANY, vmem=60)(v)
    near = lax.all_to_all(near, "px", 0, 0, tiled=True, axis_index_groups=adjacent)
    here, low, high = call(
        moments_y, [SMEM, SMEM, VMEM], [(6 * YROWS, LANES)] + [(ROWS, LANES)] * 2, 1500
    )(place, wall, v)

    def sibling_of(cube, stage):
        return lax.ppermute(cube, "pz", [(i, i ^ (1 << stage)) for i in range(pz)])

    def join_stage(stage, *arrays):
        body = functools.partial(join, stage, wall_rows)
        cube = [(6 * YROWS, LANES)] * 2
        return call(body, [VMEM] * len(arrays), cube, 200)(*arrays)

    stages = pz.bit_length() - 1
    sibling = sibling_of(here, 0)
    cube, inflow = join_stage(0, here, sibling)
    own = call(group_moments, [VMEM], [(4 * PART, LANES)], 300, after=[cube])(near)
    other = lax.ppermute(own, "px", [(i, i ^ GROUP) for i in range(px)])
    pair_chunk = (groups // 2, 4 * PART, LANES)
    far = call(
        functools.partial(pair_moments, ring),
        [VMEM] * 2,
        [pair_chunk],
        300,
        staged(pair_chunk[1:], groups // 2),
        to=ANY,
    )(own, other)
    far = lax.all_to_all(far, "px", 0, 0, tiled=True, axis_index_groups=across)

    for stage in range(1, stages):
        sibling = sibling_of(cube, stage)
        if stage < stages - 1:
            cube, inflow = join_stage(stage, cube, sibling, inflow)
    from_below = lax.ppermute(high, "px", [(i, (i + 1) % px) for i in range(px)])
    from_above = lax.ppermute(low, "px", [((i + 1) % px, i) for i in range(px)])

    back = call(
        functools.partial(entering, ring), [VMEM] * 3, [chunk], 400, staged(chunk, GROUP), to=ANY
    )(near, other, far)
    acc, u = call(
        functools.partial(local_terms, stages - 1),
        [SMEM] * 4 + [VMEM] * 6,
        [(ROWS * XB, LANES), (YB * XB, LANES)],
        5000,
        [pltpu.VMEM((2, ROWS * XB, LANES), jnp.float32), pltpu.VMEM((ROWS * XB, LANES), jnp.float32)],
        after=[back],
    )(place, wall, metric_first, metric_second, v, from_below, from_above, cube, sibling, inflow)
    back = lax.all_to_all(back, "px", 0, 0, tiled=True, axis_index_groups=adjacent)
    out = call(finish, [VMEM] * 3, [whole], 800, staged(whole, GROUP), to=ANY)(acc, u, back)
    return out.reshape(velocity.shape)


def solution(mesh):
    return jax.shard_map(
        on_device,
        mesh=mesh,
        in_specs=(P(None, "pz", "px", None), P(), P()),
        out_specs=P(None, "pz", "px", None),
        check_vma=False,
    )
```

```python
import functools
import math

import jax
import jax.numpy as jnp
import numpy as np
from jax import lax
from jax.experimental import pallas as pl
from jax.experimental.pallas import tpu as pltpu
from jax.sharding import PartitionSpec as P


FIRST_ALPHA = 0.4998
FIRST_NEAR = 2.0 * (FIRST_ALPHA + 2.0) / 3.0
FIRST_FAR = (4.0 * FIRST_ALPHA - 1.0) / 3.0
SECOND_ALPHA = 2.0 / 11.0
SECOND_NEAR = 12.0 / 11.0
SECOND_FAR = 3.0 / 11.0
VISCOSITY = 0.5

COMPS = 3
YB = 64
XB = 8
LANES = 128
ROWS = COMPS * YB
GROUP = 8
PART = ROWS // GROUP
YROWS = COMPS * XB


class Line:
    def __init__(self, alpha, stencil, sign):
        root = math.sqrt(1.0 - 4.0 * alpha * alpha)
        self.r = -2.0 * alpha / (1.0 + root)
        green = [self.r ** abs(n) / root for n in range(-4, 5)]
        reply = [sum(stencil[k + 2] * green[n + k + 4] for k in range(-2, 3)) for n in (0, 1, 2)]
        self.sign = sign
        self.mid = reply[0]
        self.up = reply[2] / self.r**2
        self.near = reply[1] - self.up * self.r


ONE = Line(
    FIRST_ALPHA,
    [-FIRST_FAR / 4, -FIRST_NEAR / 2, 0.0, FIRST_NEAR / 2, FIRST_FAR / 4],
    -1.0,
)
TWO = Line(
    SECOND_ALPHA,
    [
        SECOND_FAR / 4,
        SECOND_NEAR,
        -2.0 * SECOND_NEAR - SECOND_FAR / 2,
        SECOND_NEAR,
        SECOND_FAR / 4,
    ],
    1.0,
)
LINES = (ONE, TWO)


def ring_table(groups, cells):
    pairs = groups // 2
    table = np.zeros((groups, 4 * pairs + 16))
    for q in range(groups):
        for s, line in enumerate(LINES):
            sigma = line.r**cells
            for d in range(1, pairs + 1):
                weight = sigma ** (2 * d - 2) / (1.0 - sigma**groups)
                table[q, (2 * s) * pairs + (q // 2 - d) % pairs] += weight
                table[q, (2 * s + 1) * pairs + (q // 2 + d) % pairs] += weight
            up, down = ((1.0, sigma), (sigma, 1.0)) if q % 2 else ((sigma, 1.0), (1.0, sigma))
            low, high = ((1.0, sigma), (0.0, 1.0)) if q % 2 else ((0.0, 1.0), (1.0, sigma))
            table[q, 4 * pairs + 8 * s : 4 * pairs + 8 * s + 8] = (*up, *down, *low, *high)
    return table.astype(np.float32)


def wall_table(blocks, cells):
    stages = blocks.bit_length() - 1
    table = np.zeros((blocks, 18 * stages + 12))
    for k in range(blocks):
        for stage in range(stages):
            size = 1 << stage
            inside = k % size
            below = (k >> stage) & 1
            row = table[k, 18 * stage : 18 * stage + 18]
            for s, line in enumerate(LINES):
                rho = line.r**cells
                own, other = (1.0, rho**size) if below else (rho**size, 1.0)
                row[2 * s : 2 * s + 2] = own, other
                row[6 + 2 * s : 8 + 2 * s] = other, own
                row[12 + 2 * s] = rho**inside if below else 0.0
                row[13 + 2 * s] = 0.0 if below else rho ** (size - 1 - inside)
            row[4:6] = (1.0, 0.0) if below else (0.0, 1.0)
            row[10:12] = (0.0, 1.0) if below else (1.0, 0.0)
            row[16] = float(below and inside == 0)
            row[17] = float(not below and inside == size - 1)
        row = table[k, 18 * stages :]
        for s, line in enumerate(LINES):
            rho = line.r**cells
            eps = line.r ** (blocks * cells + 1)
            up, down = line.up, line.sign * line.up
            scale = -line.r / (1.0 - eps * eps)
            low, high = rho**k / up, rho ** (blocks - 1 - k) / down
            row[4 * s : 4 * s + 4] = (
                -scale * eps * up * low,
                scale * down * low,
                scale * up * high,
                -scale * eps * down * high,
            )
            edge = line.near / (line.up * line.r)
            row[8 + s] = edge if k == 0 else 0.0
            row[10 + s] = edge if k == blocks - 1 else 0.0
    return table.astype(np.float32)


class Chosen:
    def __init__(self, table, index):
        self.table = table
        self.here = [index == j for j in range(1, len(table))]

    def __getitem__(self, m):
        value = float(self.table[0, m])
        for here, entry in zip(self.here, self.table[1:, m]):
            value = jnp.where(here, float(entry), value)
        return value


def plane(base, index):
    return pl.ds(base + index, 8, stride=XB)


def top_half(shape):
    return lax.broadcasted_iota(jnp.int32, shape, 0) % 8 < 4


def by_line(rows, one, two):
    return jnp.where(top_half((rows, LANES)), one, two)


def moments_x(v_ref, out_hbm, out_ref, out_sems):
    def send(part):
        return pltpu.make_async_copy(out_ref.at[part], out_hbm.at[part], out_sems.at[part])

    for part in range(GROUP):
        for g in range(part * PART // 8, (part + 1) * PART // 8):
            sums = [None] * 4
            for i in range(XB):
                f = v_ref[plane(64 * g, i), :]
                for s, line in enumerate(LINES):
                    sums[2 * s] = f if i == 0 else sums[2 * s] * line.r + f
                    sums[2 * s + 1] = f if i == 0 else sums[2 * s + 1] + line.r**i * f
            for side in range(2):
                one, two = sums[side], sums[2 + side]
                tiles = (by_line(8, one, pltpu.roll(two, 4, 0)), by_line(8, pltpu.roll(one, 4, 0), two))
                for half in range(2):
                    at = 2 * PART * side + 2 * (8 * g + 4 * half - part * PART)
                    out_ref[part, at : at + 8, :] = tiles[half]
        send(part).start()
    for part in range(GROUP):
        send(part).wait()


def moments_y(place_ref, table_ref, v_ref, here_ref, low_ref, high_ref):
    k = place_ref[1]
    base = table_ref.shape[1] - 4
    for c in range(COMPS):
        sums = [None] * 4
        first = v_ref[c * YB * XB : c * YB * XB + XB, :]
        for y in range(YB):
            f = v_ref[(c * YB + y) * XB : (c * YB + y + 1) * XB, :]
            for s, line in enumerate(LINES):
                sums[2 * s] = f if y == 0 else sums[2 * s] * line.r + f
                sums[2 * s + 1] = f if y == 0 else sums[2 * s + 1] + line.r**y * f
        last = f
        for s in range(2):
            sums[2 * s] = sums[2 * s] + table_ref[k, base + 2 + s] * last
            sums[2 * s + 1] = sums[2 * s + 1] + table_ref[k, base + s] * first
        for m, value in enumerate((*sums, last, first)):
            here_ref[m * YROWS + c * XB : m * YROWS + (c + 1) * XB, :] = value
    for g in range(ROWS // 8):
        low_ref[8 * g : 8 * g + 8, :] = v_ref[plane(64 * g, 0), :]
        high_ref[8 * g : 8 * g + 8, :] = v_ref[plane(64 * g, XB - 1), :]


def values(ref, m):
    return ref[m * YROWS : (m + 1) * YROWS, :]


def entered(stage, weights, sibling_ref, so_far):
    terms = [weights[18 * stage + 12 + m] * values(sibling_ref, m) for m in range(6)]
    return terms if so_far is None else [value + term for value, term in zip(so_far, terms)]


def joined(stage, weights, cube_ref, sibling_ref):
    at = 18 * stage
    return [
        weights[at + m] * values(cube_ref, m) + weights[at + 6 + m] * values(sibling_ref, m) for m in range(6)
    ]


def join(stage, table, cube_ref, sibling_ref, *refs):
    weights = Chosen(table, lax.axis_index("pz"))
    *before, cube_out, entering_out = refs
    so_far = [values(before[0], m) for m in range(6)] if before else None
    for m, value in enumerate(joined(stage, weights, cube_ref, sibling_ref)):
        cube_out[m * YROWS : (m + 1) * YROWS, :] = value
    for m, value in enumerate(entered(stage, weights, sibling_ref, so_far)):
        entering_out[m * YROWS : (m + 1) * YROWS, :] = value


def group_moments(near_ref, out_ref):
    rho = by_line(2 * PART, ONE.r**XB, TWO.r**XB)
    up = near_ref[0, 0 : 2 * PART, :]
    down = near_ref[GROUP - 1, 2 * PART : 4 * PART, :]
    for j in range(1, GROUP):
        up = up * rho + near_ref[j, 0 : 2 * PART, :]
        down = down * rho + near_ref[GROUP - 1 - j, 2 * PART : 4 * PART, :]
    out_ref[0 : 2 * PART, :] = up
    out_ref[2 * PART : 4 * PART, :] = down


def pair_weight(weights, m):
    at = weights.table.shape[1] - 16 + m
    return by_line(2 * PART, weights[at], weights[at + 8])


def pair_moments(table, own_ref, sibling_ref, out_hbm, out_ref, sems):
    weights = Chosen(table, lax.axis_index("px") // GROUP)
    for side in range(2):
        rows = slice(2 * PART * side, 2 * PART * (side + 1))
        total = pair_weight(weights, 2 * side) * own_ref[rows, :]
        out_ref[rows, :] = total + pair_weight(weights, 2 * side + 1) * sibling_ref[rows, :]
    copies = [pltpu.make_async_copy(out_ref, out_hbm.at[j], sems.at[j]) for j in range(out_hbm.shape[0])]
    for copy in copies:
        copy.start()
    for copy in copies:
        copy.wait()


def entering(table, near_ref, sibling_ref, far_ref, out_hbm, out_ref, sems):
    weights = Chosen(table, lax.axis_index("px") // GROUP)
    pairs = far_ref.shape[0]
    rho = by_line(2 * PART, ONE.r**XB, TWO.r**XB)
    copies = [pltpu.make_async_copy(out_ref.at[j], out_hbm.at[j], sems.at[j]) for j in range(GROUP)]
    for side in range(2):
        rows = slice(2 * PART * side, 2 * PART * (side + 1))
        total = None
        for j in range(pairs):
            weight = by_line(2 * PART, weights[side * pairs + j], weights[(2 + side) * pairs + j])
            term = weight * far_ref[j, rows, :]
            total = term if total is None else total + term
        total = pair_weight(weights, 5 + 2 * side) * total
        total = total + pair_weight(weights, 4 + 2 * side) * sibling_ref[rows, :]
        for j in range(GROUP):
            here = j if side == 0 else GROUP - 1 - j
            out_ref[here, rows, :] = total
            if side == 1:
                copies[here].start()
            if j < GROUP - 1:
                total = total * rho + near_ref[here, rows, :]
    for copy in copies:
        copy.wait()


def local_terms(
    last, place_ref, table_ref, first_ref, second_ref, v_ref, low_ref, high_ref, cube_ref, sibling_ref, before_ref,
    acc_ref, u_ref, run_ref, y_ref,
):
    k = place_ref[1]
    so_far = [values(before_ref, m) for m in range(6)]
    weights = [table_ref[k, m] for m in range(table_ref.shape[1])]
    whole = joined(last, weights, cube_ref, sibling_ref)
    *starts, rows_below, rows_above = entered(last, weights, sibling_ref, so_far)
    for s in range(2):
        for side in range(2):
            for sign in range(2):
                weight = table_ref[k, 18 * (last + 1) + 4 * s + 2 * side + sign]
                starts[2 * s + side] = starts[2 * s + side] + weight * whole[2 * s + sign]

    def pick(total):
        return tuple(total[c * XB : (c + 1) * XB] for c in range(COMPS))

    def at(c, y):
        return pl.ds(pl.multiple_of((c * YB + y) * XB, XB), XB)

    def up(y, carry):
        ones, twos = carry
        new_one, new_two = [], []
        for c in range(COMPS):
            run_ref[0, at(c, y), :] = ones[c]
            run_ref[1, at(c, y), :] = twos[c]
            f = v_ref[at(c, y), :]
            new_one.append(ones[c] * ONE.r + f)
            new_two.append(twos[c] * TWO.r + f)
        return (tuple(new_one), tuple(new_two))

    lax.fori_loop(0, YB, up, (pick(starts[0]), pick(starts[2])), unroll=8)

    below = pick(rows_below)

    def down(step, carry):
        ones, twos, after, here = carry
        y = YB - 1 - step
        slope = first_ref[k * YB + y]
        curve = VISCOSITY * second_ref[k * YB + y]
        bend = VISCOSITY * slope * slope
        factor = curve - slope * here[1]
        new_one, new_two, before_all = [], [], []
        for c in range(COMPS):
            f = here[c]
            prior = jnp.maximum(y - 1, 0)
            before = jnp.where(y > 0, v_ref[at(c, prior), :], below[c])
            run_one = run_ref[0, at(c, y), :]
            run_two = run_ref[1, at(c, y), :]
            eta_one = (ONE.up * ONE.r) * (run_one - ones[c]) + ONE.near * (before - after[c])
            eta_two = (TWO.up * TWO.r) * (run_two + twos[c]) + TWO.near * (before + after[c]) + TWO.mid * f
            y_ref[at(c, y), :] = factor * eta_one + bend * eta_two
            new_one.append(ones[c] * ONE.r + f)
            new_two.append(twos[c] * TWO.r + f)
            before_all.append(before)
        return (tuple(new_one), tuple(new_two), here, tuple(before_all))

    top = tuple(v_ref[(c * YB + YB - 1) * XB : (c * YB + YB) * XB, :] for c in range(COMPS))
    lax.fori_loop(
        0, YB, down, (pick(starts[1]), pick(starts[3]), pick(rows_above), top), unroll=8
    )

    for g in range(ROWS // 8):
        f = [v_ref[plane(64 * g, i), :] for i in range(XB)]
        rows = slice(8 * g, 8 * g + 8)
        ext = [low_ref[rows, :]] + f + [high_ref[rows, :]]
        runs = []
        for line in LINES:
            left, right = [None], [None]
            for i in range(XB - 1):
                left.append(f[i] if i == 0 else left[-1] * line.r + f[i])
                right.append(f[XB - 1 - i] if i == 0 else right[-1] * line.r + f[XB - 1 - i])
            runs.append((left, right[::-1]))
        for i in range(XB):
            pair_one = ONE.near * (ext[i] - ext[i + 2])
            pair_two = (VISCOSITY * TWO.near) * (ext[i] + ext[i + 2]) + (VISCOSITY * TWO.mid) * f[i]
            (left, right), (left_two, right_two) = runs
            for value, sign in ((left[i], 1.0), (right[i], -1.0)):
                if value is not None:
                    pair_one = pair_one + (sign * ONE.up * ONE.r) * value
            for value in (left_two[i], right_two[i]):
                if value is not None:
                    pair_two = pair_two + (VISCOSITY * TWO.up * TWO.r) * value
            u = v_ref[plane(64 * (g % 8), i), :]
            if g < 8:
                u_ref[64 * g + 8 * i : 64 * g + 8 * i + 8, :] = u
            total = y_ref[plane(64 * g, i), :] - u * pair_one + pair_two
            acc_ref[64 * g + 8 * i : 64 * g + 8 * i + 8, :] = total


def finish(acc_ref, u_ref, far_ref, out_hbm, out_ref, sems):
    count = sems.shape[0]
    groups = ROWS // 8 // count

    def send(piece):
        rows = pl.ds(piece * groups * 64, groups * 64)
        return pltpu.make_async_copy(out_ref.at[rows], out_hbm.at[rows], sems.at[piece])

    for g in range(ROWS // 8):
        sums = []
        for side in range(2):
            tiles = []
            for half in range(2):
                part, at = divmod(8 * g + 4 * half, PART)
                at = 2 * PART * side + 2 * at
                tiles.append(far_ref[part, at : at + 8, :])
            sums.append(by_line(8, tiles[0], pltpu.roll(tiles[1], 4, 0)))
            sums.append(by_line(8, pltpu.roll(tiles[0], 4, 0), tiles[1]))
        left_one, left_two, right_one, right_two = sums
        for i in range(XB):
            one = (ONE.up * ONE.r ** (i + 1)) * left_one - (ONE.up * ONE.r ** (XB - i)) * right_one
            two = (VISCOSITY * TWO.up * TWO.r ** (i + 1)) * left_two
            two = two + (VISCOSITY * TWO.up * TWO.r ** (XB - i)) * right_two
            u = u_ref[64 * (g % 8) + 8 * i : 64 * (g % 8) + 8 * i + 8, :]
            acc = acc_ref[64 * g + 8 * i : 64 * g + 8 * i + 8, :]
            out_ref[plane(64 * g, i), :] = (acc + two) - u * one
        if (g + 1) % groups == 0:
            send(g // groups).start()
    for piece in range(count):
        send(piece).wait()


VMEM = pl.BlockSpec(memory_space=pltpu.VMEM)
SMEM = pl.BlockSpec(memory_space=pltpu.SMEM)
ANY = pl.BlockSpec(memory_space=pl.ANY)


def staged(shape, *counts):
    return [pltpu.VMEM(shape, jnp.float32)] + [pltpu.SemaphoreType.DMA((n,)) for n in counts]


def call(body, ins, outs, cycles, scratch=(), after=(), to=None, vmem=12):
    count = len(ins)

    def placed(*refs):
        body(*refs[:count], *refs[count + len(after) :])

    shapes = tuple(jax.ShapeDtypeStruct(s, jnp.float32) for s in outs)
    moved = 4 * sum(math.prod(s) for s in outs)
    kernel = pl.pallas_call(
        placed,
        out_shape=shapes if len(shapes) > 1 else shapes[0],
        in_specs=list(ins) + [pl.BlockSpec(memory_space=pl.ANY)] * len(after),
        out_specs=tuple(to or VMEM for _ in outs) if len(outs) > 1 else to or VMEM,
        scratch_shapes=list(scratch),
        compiler_params=pltpu.CompilerParams(vmem_limit_bytes=vmem << 20),
        cost_estimate=pl.CostEstimate(flops=cycles * 1024, bytes_accessed=2 * moved, transcendentals=0),
    )

    def run(*arrays):
        return kernel(*arrays, *after)

    return run


def on_device(velocity, metric_first, metric_second):
    px = lax.axis_size("px")
    pz = lax.axis_size("pz")
    groups = px // GROUP
    adjacent = [[GROUP * q + j for j in range(GROUP)] for q in range(groups)]
    across = [[j + 2 * GROUP * q for q in range(groups // 2)] for j in range(2 * GROUP)]
    place = jnp.stack([lax.axis_index("px") // GROUP, lax.axis_index("pz")]).astype(jnp.int32)
    ring = ring_table(groups, GROUP * XB)
    wall_rows = wall_table(pz, YB)
    wall = jnp.asarray(wall_rows)
    chunk = (GROUP, 4 * PART, LANES)
    v = velocity.reshape(ROWS * XB, LANES)

    whole = (ROWS * XB, LANES)
    near = call(moments_x, [VMEM], [chunk], 1500, staged(chunk, GROUP), to=ANY)(v)
    near = lax.all_to_all(near, "px", 0, 0, tiled=True, axis_index_groups=adjacent)
    here, low, high = call(
        moments_y, [SMEM, SMEM, VMEM], [(6 * YROWS, LANES)] + [(ROWS, LANES)] * 2, 1500
    )(place, wall, v)

    def sibling_of(cube, stage):
        return lax.ppermute(cube, "pz", [(i, i ^ (1 << stage)) for i in range(pz)])

    def join_stage(stage, *arrays):
        body = functools.partial(join, stage, wall_rows)
        cube = [(6 * YROWS, LANES)] * 2
        return call(body, [VMEM] * len(arrays), cube, 200)(*arrays)

    stages = pz.bit_length() - 1
    sibling = sibling_of(here, 0)
    cube, inflow = join_stage(0, here, sibling)
    own = call(group_moments, [VMEM], [(4 * PART, LANES)], 300, after=[cube])(near)
    other = lax.ppermute(own, "px", [(i, i ^ GROUP) for i in range(px)])
    pair_chunk = (groups // 2, 4 * PART, LANES)
    far = call(
        functools.partial(pair_moments, ring),
        [VMEM] * 2,
        [pair_chunk],
        300,
        staged(pair_chunk[1:], groups // 2),
        to=ANY,
    )(own, other)
    far = lax.all_to_all(far, "px", 0, 0, tiled=True, axis_index_groups=across)

    for stage in range(1, stages):
        sibling = sibling_of(cube, stage)
        if stage < stages - 1:
            cube, inflow = join_stage(stage, cube, sibling, inflow)
    from_below = lax.ppermute(high, "px", [(i, (i + 1) % px) for i in range(px)])
    from_above = lax.ppermute(low, "px", [((i + 1) % px, i) for i in range(px)])

    back = call(
        functools.partial(entering, ring), [VMEM] * 3, [chunk], 400, staged(chunk, GROUP), to=ANY
    )(near, other, far)
    acc, u = call(
        functools.partial(local_terms, stages - 1),
        [SMEM] * 4 + [VMEM] * 6,
        [(ROWS * XB, LANES), (YB * XB, LANES)],
        5000,
        [pltpu.VMEM((2, ROWS * XB, LANES), jnp.float32), pltpu.VMEM((ROWS * XB, LANES), jnp.float32)],
        after=[back],
    )(place, wall, metric_first, metric_second, v, from_below, from_above, cube, sibling, inflow)
    back = lax.all_to_all(back, "px", 0, 0, tiled=True, axis_index_groups=adjacent)
    out = call(finish, [VMEM] * 3, [whole], 800, staged(whole, 12), to=ANY)(acc, u, back)
    return out.reshape(velocity.shape)


def solution(mesh):
    return jax.shard_map(
        on_device,
        mesh=mesh,
        in_specs=(P(None, "pz", "px", None), P(), P()),
        out_specs=P(None, "pz", "px", None),
        check_vma=False,
    )
```
